512 devices in a mesh: node: 64 (over y, z_lo, core), local: 8 (over z_hi, x).
Axes of the slice: x: 4, y: 8, z: 8 (z_hi: 2, z_lo: 4; z = z_hi * 4 + z_lo), core: 2. Of those that a mesh axis runs over, the one named last changes fastest.
Arguments:
- hidden_acts: bfloat16 [65536, 1024], P(('node', 'local')), may hold values from -6 to 6
- out_grad: bfloat16 [65536, 4096], P(('node', 'local')), may hold values from -6 to 6
- weight: bfloat16 [32768, 4096], P('node', 'local'), may hold values from -0.1875 to 0.1875
- first_moment: bfloat16 [32768, 4096], P('node', 'local'), may hold values from -6 to 6
- second_moment: bfloat16 [32768, 4096], P('node', 'local'), may hold values from 0.5 to 8
- holder_expert: int32 [32], replicated, may hold values from 0 to 31
- new_source: int32 [32], replicated, may hold values from 0 to 31, as said below
- live_blocks: int32 [64, 8], P('node', 'local'), may hold values from 1 to 4, as said below
Outputs:
- next_weight: bfloat16 [32768, 4096], P('node', 'local')
- next_first: bfloat16 [32768, 4096], P('node', 'local')
- next_second: bfloat16 [32768, 4096], P('node', 'local')
- hidden_back: bfloat16 [65536, 1024], P(('node', 'local'))
The draws below stay inside these ranges and needn't reach their ends.
Inputs may be any that keep to these rules, and one draw needn't show every extreme that they name: `new_source`: each entry names a copy. The live rows of a device are its first 32 * live_blocks rows.
All inputs are finite; a program needn't handle non-finite values.
Results may differ from the reference program's by a relative error of at most 0.001.
Values may be sent and summed in bfloat16 or wider, within the bound.
A program may use at most 64 MiB of HBM per device.

```python
import math
import jax
import jax.numpy as jnp
import numpy as np
from jax import lax

D = 4096
H = 1024
TOK_DEV = 128
ROW_BLOCK = 32
COPIES = 32
TOKENS = 65536
N_NODE = 64
N_LOCAL = 8


def draw_live_blocks(key, part):
    most = TOK_DEV // ROW_BLOCK
    counts = jax.random.randint(key, (N_NODE, N_LOCAL), 1, most + 1, dtype=jnp.int32)
    return counts.at[0, 0].set(most).at[0, 1].set(1)


def draw_new_source(key, part):
    key_move, key_from = jax.random.split(jax.random.fold_in(key, 7))
    own_index = jnp.arange(COPIES, dtype=jnp.int32)
    moving = jax.random.randint(key_move, (COPIES,), 0, 4, dtype=jnp.int32) == 0
    sources = jax.random.randint(key_from, (COPIES,), 0, COPIES, dtype=jnp.int32)
    picked = jnp.where(moving, sources, own_index)
    return picked.at[0].set(COPIES - 1).at[1].set(0)


def touch_ends(drawn, key, least, largest):
    dims = drawn.shape
    place = [jax.random.randint(jax.random.fold_in(key, axis), (), 0, dims[axis]) for axis in range(len(dims))]
    drawn = drawn.at[tuple(place)].set(least)
    longest = dims.index(max(dims))
    place[longest] = (place[longest] + 1) % dims[longest]
    return drawn.at[tuple(place)].set(largest)


def levels(own_key, dims, pieces, low, high):
    factor_of, own = 1.0, jax.random.fold_in(own_key, 6)
    for position, blocks in pieces:
        draws = jnp.exp(jax.random.uniform(jax.random.fold_in(own, position), (blocks,), jnp.float32, low / len(pieces), high / len(pieces)))
        factor_of = factor_of * jnp.repeat(draws, dims[position] // blocks).reshape([-1 if axis == position else 1 for axis in range(len(dims))])
    return factor_of


def rank_table(amount, lean):
    portions = [(1 << 20) // math.isqrt(rank ** lean) + 1 for rank in range(1, amount + 1)]
    scale = 1 + sum(portions) // (1 << 30)
    return np.cumsum(np.array([max(1, weight // scale) for weight in portions]))


def ranked(own_key, shape, number_of, slope):
    grid = rank_table(number_of, slope)
    ticket = jax.random.randint(jax.random.fold_in(own_key, 1), shape, 0, int(grid[number_of - 1]))
    grade = jnp.searchsorted(jnp.asarray(grid, jnp.int32), ticket, side="right")
    return jax.random.permutation(jax.random.fold_in(own_key, 2), number_of)[grade].astype(jnp.int32)


def normal_values(rng, dims, width, bound, pieces=(), kind=jnp.bfloat16):
    loudness = levels(rng, dims, pieces, -0.22, 0.18) if pieces else 1.0
    array = jax.random.normal(rng, dims, jnp.float32) * width * loudness
    return jnp.minimum(jnp.maximum(array, -bound), bound).astype(kind)


def setup_inputs(seed: int = 0) -> dict:
    splits = jax.random.split(jax.random.key(seed), 9)
    hidden_acts = normal_values(splits[0], (TOKENS, H), 1.0, 6.0, ((0, 512),))
    out_grad = normal_values(splits[1], (TOKENS, D), 1.0, 6.0, ((0, 512),))
    weight = normal_values(splits[2], (COPIES * H, D), H ** -0.5, 0.1875, ((0, 64), (1, 8)))
    first_moment = normal_values(splits[3], (COPIES * H, D), 1.0, 6.0, ((0, 64), (1, 8)))
    second_moment = jnp.clip(jnp.exp(math.log(8.0) - 2.7725887 * jax.random.uniform(splits[4], (COPIES * H, D), jnp.float32) ** levels(splits[4], (COPIES * H, D), ((0, 64), (1, 8)), -0.2, 0.2)), 0.5, 8.0).astype(jnp.bfloat16)
    holder_expert = touch_ends(ranked(splits[5], (COPIES,), COPIES, 2), jax.random.fold_in(splits[5], 3), 0, COPIES - 1).astype(jnp.int32)
    new_source = draw_new_source(jax.random.fold_in(splits[8], 71), 0)
    live_blocks = draw_live_blocks(jax.random.fold_in(splits[8], 71), 0)
    return {"hidden_acts": hidden_acts, "out_grad": out_grad, "weight": weight, "first_moment": first_moment, "second_moment": second_moment, "holder_expert": holder_expert, "new_source": new_source, "live_blocks": live_blocks}


beta_one = 0.9
beta_two = 0.95
learn_rate = 0.002
decay_rate = 0.1
adam_eps = 1e-08
step_count = 10.0

def adamw_step(gradient, weight, first, second):
    first_new = beta_one * first.astype(jnp.float32) + (1.0 - beta_one) * gradient
    second_new = beta_two * second.astype(jnp.float32) + (1.0 - beta_two) * gradient * gradient
    update = first_new / (1.0 - beta_one ** step_count) / (jnp.sqrt(second_new / (1.0 - beta_two ** step_count)) + adam_eps)
    master = weight.astype(jnp.float32)
    weight_new = master - learn_rate * (update + decay_rate * master)
    return (weight_new.astype(jnp.bfloat16), first_new.astype(jnp.bfloat16), second_new.astype(jnp.bfloat16))

def reference(hidden_acts, out_grad, weight, first_moment, second_moment, holder_expert, new_source, live_blocks):
    copy_count = holder_expert.shape[0]
    row_ids = jnp.arange(TOK_DEV, dtype=jnp.int32)
    limits = (live_blocks * ROW_BLOCK).reshape(-1)
    live_mask = (row_ids[None, :] < limits[:, None]).reshape(-1, 1)
    masked = jnp.where(live_mask, out_grad, jnp.zeros_like(out_grad))
    copy_hidden = hidden_acts.reshape(copy_count, -1, H)
    copy_grad = masked.reshape(copy_count, -1, D)
    copy_weight = weight.reshape(copy_count, H, D)

    def copy_terms(operands):
        hidden_rows, grad_rows, weight_rows = operands
        gradient = lax.dot_general(hidden_rows, grad_rows, (((0,), (0,)), ((), ())), preferred_element_type=jnp.float32)
        back = lax.dot_general(grad_rows, weight_rows, (((1,), (1,)), ((), ())), preferred_element_type=jnp.float32)
        return (gradient, back.astype(jnp.bfloat16))
    gradients, hidden_back = lax.map(copy_terms, (copy_hidden, copy_grad, copy_weight))
    group_blend = (holder_expert[:, None] == holder_expert[None, :]).astype(jnp.float32)
    summed = jnp.einsum('kj,jhd->khd', group_blend, gradients, precision=lax.Precision.HIGHEST)
    weight_new, first_new, second_new = adamw_step(summed, copy_weight, first_moment.reshape(copy_count, H, D), second_moment.reshape(copy_count, H, D))
    return (jnp.take(weight_new, new_source, axis=0).reshape(-1, D), jnp.take(first_new, new_source, axis=0).reshape(-1, D), jnp.take(second_new, new_source, axis=0).reshape(-1, D), hidden_back.reshape(-1, H))
```

```python
import functools

import jax
import jax.numpy as jnp
from jax import lax
from jax.experimental import pallas as pl
from jax.experimental.pallas import tpu as pltpu
from jax.sharding import PartitionSpec as P

ROW_BLOCK = 32
MESH = pl.DeviceIdType.MESH

beta_one = 0.9
beta_two = 0.95
learn_rate = 0.002
decay_rate = 0.1
adam_eps = 1e-08
step_count = 10.0


def adamw_step(gradient, weight, first, second):
    first_new = beta_one * first + (1.0 - beta_one) * gradient
    second_new = beta_two * second + (1.0 - beta_two) * gradient * gradient
    update = (
        first_new
        / (1.0 - beta_one**step_count)
        / (jnp.sqrt(second_new / (1.0 - beta_two**step_count)) + adam_eps)
    )
    weight_new = weight - learn_rate * (update + decay_rate * weight)
    return weight_new, first_new, second_new


def step_kernel(
    copies,
    ring,
    live_ref,
    holder_ref,
    source_ref,
    hid_ref,
    og_ref,
    w_ref,
    m1_ref,
    m2_ref,
    nw_ref,
    nf_ref,
    ns_ref,
    hb_ref,
    hid_m,
    hbuf,
    gbuf,
    sbuf,
    wbuf,
    gsend,
    grecv,
    gsum,
    sout,
    part,
    precv,
    back,
    brecv,
    og_send,
    og_recv,
    hid_send,
    hid_recv,
    fwd_send,
    fwd_recv,
    in_send,
    in_recv,
    w_send,
    w_recv,
    g_send,
    g_recv,
    p_send,
    p_recv,
    b_send,
    b_recv,
    out_send,
    out_recv,
):
    tok = hid_ref.shape[0]
    rows, cols = w_ref.shape
    piece = rows // copies
    half = ring * tok
    node = lax.axis_index("node")
    local = lax.axis_index("local")
    c, p = node // 2, node % 2
    zh, x = local // ring, local % ring

    def remote(src, dst, send, recv, where):
        pltpu.make_async_remote_copy(
            src_ref=src,
            dst_ref=dst,
            send_sem=send,
            recv_sem=recv,
            device_id=where,
            device_id_type=MESH,
        ).start()

    def wait(ref, sem):
        pltpu.make_async_copy(ref, ref, sem).wait()

    def lanes(start, size):
        return pl.ds(pl.multiple_of(start, 128), size)

    def span(start, size):
        return pl.ds(pl.multiple_of(start, 16), size)

    def other(k):
        return (c + 13 * k) % copies

    def greet(where):
        pl.semaphore_signal(barrier, inc=1, device_id=where, device_id_type=MESH)

    hops = [dx for pair in zip(range(1, ring), range(ring - 1, 0, -1)) for dx in pair]
    hops = list(dict.fromkeys(hops))
    states = (w_ref, m1_ref, m2_ref)
    outs = (nw_ref, nf_ref, ns_ref)
    mine = span((p * ring + x) * tok, tok)

    barrier = pltpu.get_barrier_semaphore()

    def greet_far(k, carry):
        greet((2 * other(k) + p, (1 - zh) * ring + x))
        return carry

    def greet_near(k, carry):
        greet((2 * other(k) + p, local))
        return carry

    lax.fori_loop(0, copies, greet_far, 0)
    lax.fori_loop(1, copies, greet_near, 0)
    for dx in hops:
        for q in range(2):
            greet((2 * c + q, zh * ring + (x + dx) % ring))
    greet((2 * c + 1 - p, local))

    live = live_ref[0, 0] * ROW_BLOCK
    alive = lax.broadcasted_iota(jnp.int32, (tok, 1), 0) < live
    hid_m[...] = jnp.where(alive, hid_ref[...], jnp.zeros_like(hid_ref))
    for b in range(2):
        pltpu.make_async_copy(
            og_ref.at[:, lanes((b * ring + x) * cols, cols)],
            gbuf.at[mine, pl.ds(b * cols, cols)],
            og_recv.at[0],
        ).start()
    for a in range(3):
        pltpu.make_async_copy(
            states[a].at[span(c * piece, piece)], sbuf.at[a, c], in_recv
        ).start()
    pl.semaphore_wait(barrier, 2 * copies + 2 * (ring - 1))

    for dx in hops:
        there = zh * ring + (x + dx) % ring
        for b in range(2):
            remote(
                og_ref.at[:, lanes((b * ring + (x + dx) % ring) * cols, cols)],
                gbuf.at[mine, pl.ds(b * cols, cols)],
                og_send,
                og_recv.at[dx],
                (node, there),
            )
        for q in range(2):
            remote(
                hid_m.at[:, pl.ds(q * rows, rows)],
                hbuf.at[mine],
                hid_send,
                hid_recv,
                (2 * c + q, there),
            )
    remote(
        hid_m.at[:, lanes((1 - p) * rows, rows)],
        hbuf.at[mine],
        hid_send,
        hid_recv,
        (2 * c + 1 - p, local),
    )
    pltpu.make_async_copy(
        hid_m.at[:, lanes(p * rows, rows)], hbuf.at[mine], hid_recv
    ).start()

    def send_states(k, carry):
        there = other(k)
        for a in range(3):
            remote(
                states[a].at[span(there * piece, piece)],
                sbuf.at[a, c],
                in_send,
                in_recv,
                (2 * there + p, local),
            )
        return carry

    lax.fori_loop(1, copies, send_states, 0)

    for dx in [0] + hops:
        theirs = span((p * ring + (x + ring - dx) % ring) * tok, tok)
        wait(gbuf.at[theirs], og_recv.at[dx])
        remote(
            gbuf.at[theirs],
            gbuf.at[theirs],
            fwd_send,
            fwd_recv,
            (2 * c + 1 - p, local),
        )
    wait(hbuf, hid_recv)
    wait(gbuf.at[span((1 - p) * half, half)], fwd_recv)

    chunk = min(128, rows)
    many = rows // chunk
    group = chunk // piece

    def turn(r):
        return (c // group + r) % many

    def grad_chunk(r):
        at = turn(r)
        acc = lax.dot_general(
            hbuf[:, lanes(at * chunk, chunk)],
            gbuf[...],
            (((0,), (0,)), ((), ())),
            preferred_element_type=jnp.float32,
        )
        for b in range(2):
            for j in range(group):
                gsend[b * copies + at * group + j] = acc[
                    j * piece : (j + 1) * piece, b * cols : (b + 1) * cols
                ]

    def grad_send(r):
        at = turn(r)

        def one(i, carry):
            there = at * group + (c + i) % group
            for flip in (1, 0):
                b = (zh + flip) % 2
                to_self = (there == c) & (flip == 0)
                slot = gsend.at[b * copies + there]
                home = grecv.at[zh * copies + c]

                @pl.when(jnp.logical_not(to_self))
                def _():
                    remote(slot, home, g_send, g_recv, (2 * there + p, b * ring + x))

                if flip == 0:

                    @pl.when(to_self)
                    def _():
                        pltpu.make_async_copy(slot, home, g_recv).start()

            return carry

        lax.fori_loop(0, group, one, 0)

    for r in range(many):
        grad_chunk(r)
        if r >= 1:
            grad_send(r - 1)
    remote(
        w_ref,
        wbuf.at[:, lanes(zh * cols, cols)],
        w_send,
        w_recv.at[1],
        (node, (1 - zh) * ring + x),
    )
    pltpu.make_async_copy(
        w_ref, wbuf.at[:, lanes(zh * cols, cols)], w_recv.at[0]
    ).start()
    grad_send(many - 1)

    wait(sbuf, in_recv)
    wait(grecv, g_recv)

    def add_halves(j, carry):
        gsum[j] = grecv[j] + grecv[copies + j]
        return carry

    lax.fori_loop(0, copies, add_halves, 0)

    def update(k):
        there = other(k)
        src = source_ref[there]
        expert = holder_ref[src]

        def add(j, total):
            return total + jnp.where(holder_ref[j] == expert, 1.0, 0.0) * gsum[j]

        total = lax.fori_loop(
            0, copies, add, jnp.zeros((piece, cols), jnp.float32), unroll=4
        )
        new = adamw_step(
            total,
            sbuf[0, src].astype(jnp.float32),
            sbuf[1, src].astype(jnp.float32),
            sbuf[2, src].astype(jnp.float32),
        )
        for a in range(3):
            sout[a, there] = new[a].astype(jnp.bfloat16)

    def send_update(k):
        there = other(k)
        for a in range(3):
            remote(
                sout.at[a, there],
                outs[a].at[span(c * piece, piece)],
                out_send,
                out_recv.at[a],
                (2 * there + p, local),
            )

    update(1)

    def update_step(k, carry):
        update(k)
        send_update(k - 1)
        return carry

    lax.fori_loop(2, copies, update_step, 0)
    update(0)
    send_update(copies - 1)

    for b in range(2):
        wait(wbuf.at[:, pl.ds(b * cols, cols)], w_recv.at[b])
    for a in range(3):
        pltpu.make_async_copy(
            sout.at[a, c], outs[a].at[span(c * piece, piece)], out_recv.at[a]
        ).start()
    block = min(256, 2 * half)

    def back_chunk(i, carry):
        here = span(i * block, block)
        part[here] = lax.dot_general(
            gbuf[here],
            wbuf[...],
            (((1,), (1,)), ((), ())),
            preferred_element_type=jnp.float32,
        )
        return carry

    lax.fori_loop(0, 2 * half // block, back_chunk, 0)
    for dx in hops:
        xx = (x + dx) % ring
        for q in range(2):
            remote(
                part.at[span((q * ring + xx) * tok, tok)],
                precv.at[dx - 1, q],
                p_send,
                p_recv,
                (node, zh * ring + xx),
            )
    wait(precv, p_recv)

    def summed(q):
        total = part[span((q * ring + x) * tok, tok)]
        for dx in hops:
            total = total + precv[dx - 1, q]
        return total.astype(jnp.bfloat16)

    back[...] = summed(1 - p)
    own = summed(p)
    hb_ref[:, lanes(p * rows, rows)] = jnp.where(alive, own, jnp.zeros_like(own))
    remote(back, brecv, b_send, b_recv, (2 * c + 1 - p, local))
    wait(brecv, b_recv)
    rest = brecv[...]
    hb_ref[:, lanes((1 - p) * rows, rows)] = jnp.where(alive, rest, jnp.zeros_like(rest))

    for a in range(3):
        wait(outs[a], out_recv.at[a])
    wait(gbuf.at[span(0, (ring - 1) * tok)], og_send)
    wait(hbuf.at[span(0, (2 * ring - 1) * tok)], hid_send)
    wait(gbuf.at[span(0, half)], fwd_send)
    wait(sbuf.at[:, pl.ds(0, copies - 1)], in_send)
    wait(wbuf.at[:, pl.ds(0, cols)], w_send)
    wait(gsend.at[pl.ds(0, 2 * copies - 1)], g_send)
    wait(sout.at[:, pl.ds(0, copies - 1)], out_send)
    wait(precv, p_send)
    wait(brecv, b_send)


def shards(hidden_acts, out_grad, weight, first, second, holder, source, live):
    copies = lax.axis_size("node") // 2
    ring = lax.axis_size("local") // 2
    tok, hid = hidden_acts.shape
    rows, cols = weight.shape
    piece = rows // copies
    half = ring * tok
    smem = pl.BlockSpec(memory_space=pltpu.SMEM)
    vmem = pl.BlockSpec(memory_space=pltpu.VMEM)
    far = pl.BlockSpec(memory_space=pl.ANY)
    dma = pltpu.SemaphoreType.DMA
    bf16, f32 = jnp.bfloat16, jnp.float32
    state = jax.ShapeDtypeStruct((rows, cols), bf16)
    return pl.pallas_call(
        functools.partial(step_kernel, copies, ring),
        out_shape=(state, state, state, jax.ShapeDtypeStruct((tok, hid), bf16)),
        in_specs=[smem, smem, smem, vmem, far, far, far, far],
        out_specs=(far, far, far, vmem),
        scratch_shapes=[
            pltpu.VMEM((tok, hid), bf16),
            pltpu.VMEM((2 * half, rows), bf16),
            pltpu.VMEM((2 * half, 2 * cols), bf16),
            pltpu.VMEM((3, copies, piece, cols), bf16),
            pltpu.VMEM((rows, 2 * cols), bf16),
            pltpu.VMEM((2 * copies, piece, cols), f32),
            pltpu.VMEM((2 * copies, piece, cols), f32),
            pltpu.VMEM((copies, piece, cols), f32),
            pltpu.VMEM((3, copies, piece, cols), bf16),
            pltpu.VMEM((2 * half, rows), f32),
            pltpu.VMEM((ring - 1, 2, tok, rows), f32),
            pltpu.VMEM((tok, rows), bf16),
            pltpu.VMEM((tok, rows), bf16),
            dma,
            dma((ring,)),
            dma,
            dma,
            dma,
            dma,
            dma,
            dma,
            dma,
            dma((2,)),
            dma,
            dma,
            dma,
            dma,
            dma,
            dma,
            dma,
            dma((3,)),
        ],
        compiler_params=pltpu.CompilerParams(
            collective_id=0, has_side_effects=True, vmem_limit_bytes=40 * 1024 * 1024
        ),
    )(live, holder, source, hidden_acts, out_grad, weight, first, second)


def solution(mesh):
    token, split = P(("node", "local"), None), P("node", "local")
    return jax.shard_map(
        shards,
        mesh=mesh,
        in_specs=(token, token, split, split, split, P(), P(), split),
        out_specs=(split, split, split, token),
        check_vma=False,
    )
```

```python
import functools

import jax
import jax.numpy as jnp
from jax import lax
from jax.experimental import pallas as pl
from jax.experimental.pallas import tpu as pltpu
from jax.sharding import PartitionSpec as P

ROW_BLOCK = 32
MESH = pl.DeviceIdType.MESH

beta_one = 0.9
beta_two = 0.95
learn_rate = 0.002
decay_rate = 0.1
adam_eps = 1e-08
step_count = 10.0


def adamw_step(gradient, weight, first, second):
    first_new = beta_one * first + (1.0 - beta_one) * gradient
    second_new = beta_two * second + (1.0 - beta_two) * gradient * gradient
    update = (
        first_new
        / (1.0 - beta_one**step_count)
        / (jnp.sqrt(second_new / (1.0 - beta_two**step_count)) + adam_eps)
    )
    weight_new = weight - learn_rate * (update + decay_rate * weight)
    return weight_new, first_new, second_new


def step_kernel(
    copies,
    ring,
    live_ref,
    holder_ref,
    source_ref,
    hid_ref,
    og_ref,
    w_ref,
    m1_ref,
    m2_ref,
    nw_ref,
    nf_ref,
    ns_ref,
    hb_ref,
    hid_m,
    hbuf,
    gbuf,
    sbuf,
    wbuf,
    gsend,
    grecv,
    qsend,
    qrecv,
    gsum,
    sout,
    part,
    precv,
    back,
    brecv,
    og_send,
    og_recv,
    hid_send,
    hid_recv,
    fwd_send,
    fwd_recv,
    in_send,
    in_recv,
    w_send,
    w_recv,
    g_send,
    g_recv,
    q_send,
    q_recv,
    p_send,
    p_recv,
    b_send,
    b_recv,
    out_send,
    out_recv,
):
    tok = hid_ref.shape[0]
    rows, cols = w_ref.shape
    piece = rows // copies
    half = ring * tok
    node = lax.axis_index("node")
    local = lax.axis_index("local")
    c, p = node // 2, node % 2
    zh, x = local // ring, local % ring

    def remote(src, dst, send, recv, where):
        pltpu.make_async_remote_copy(
            src_ref=src,
            dst_ref=dst,
            send_sem=send,
            recv_sem=recv,
            device_id=where,
            device_id_type=MESH,
        ).start()

    def wait(ref, sem):
        pltpu.make_async_copy(ref, ref, sem).wait()

    def lanes(start, size):
        return pl.ds(pl.multiple_of(start, 128), size)

    def span(start, size):
        return pl.ds(pl.multiple_of(start, 16), size)

    def other(k):
        return (c + 13 * k) % copies

    def greet(where):
        pl.semaphore_signal(barrier, inc=1, device_id=where, device_id_type=MESH)

    hops = [dx for pair in zip(range(1, ring), range(ring - 1, 0, -1)) for dx in pair]
    hops = list(dict.fromkeys(hops))
    states = (w_ref, m1_ref, m2_ref)
    outs = (nw_ref, nf_ref, ns_ref)
    mine = span((p * ring + x) * tok, tok)

    barrier = pltpu.get_barrier_semaphore()

    def greet_far(k, carry):
        greet((2 * other(k) + p, (1 - zh) * ring + x))
        return carry

    def greet_near(k, carry):
        greet((2 * other(k) + p, local))
        return carry

    lax.fori_loop(0, copies, greet_far, 0)
    lax.fori_loop(1, copies, greet_near, 0)
    for dx in hops:
        for q in range(2):
            greet((2 * c + q, zh * ring + (x + dx) % ring))
    greet((2 * c + 1 - p, local))

    live = live_ref[0, 0] * ROW_BLOCK
    alive = lax.broadcasted_iota(jnp.int32, (tok, 1), 0) < live
    hid_m[...] = jnp.where(alive, hid_ref[...], jnp.zeros_like(hid_ref))
    for b in range(2):
        pltpu.make_async_copy(
            og_ref.at[:, lanes((b * ring + x) * cols, cols)],
            gbuf.at[mine, pl.ds(b * cols, cols)],
            og_recv.at[0],
        ).start()
    for a in range(3):
        pltpu.make_async_copy(
            states[a].at[span(c * piece, piece)], sbuf.at[a, c], in_recv
        ).start()
    pl.semaphore_wait(barrier, 2 * copies + 2 * (ring - 1))

    for dx in hops:
        there = zh * ring + (x + dx) % ring
        for b in range(2):
            remote(
                og_ref.at[:, lanes((b * ring + (x + dx) % ring) * cols, cols)],
                gbuf.at[mine, pl.ds(b * cols, cols)],
                og_send,
                og_recv.at[dx],
                (node, there),
            )
        for q in range(2):
            remote(
                hid_m.at[:, pl.ds(q * rows, rows)],
                hbuf.at[mine],
                hid_send,
                hid_recv,
                (2 * c + q, there),
            )
    remote(
        hid_m.at[:, lanes((1 - p) * rows, rows)],
        hbuf.at[mine],
        hid_send,
        hid_recv,
        (2 * c + 1 - p, local),
    )
    pltpu.make_async_copy(
        hid_m.at[:, lanes(p * rows, rows)], hbuf.at[mine], hid_recv
    ).start()

    def send_states(k, carry):
        there = other(k)
        for a in range(3):
            remote(
                states[a].at[span(there * piece, piece)],
                sbuf.at[a, c],
                in_send,
                in_recv,
                (2 * there + p, local),
            )
        return carry

    lax.fori_loop(1, copies, send_states, 0)

    for dx in [0] + hops:
        theirs = span((p * ring + (x + ring - dx) % ring) * tok, tok)
        wait(gbuf.at[theirs], og_recv.at[dx])
        remote(
            gbuf.at[theirs],
            gbuf.at[theirs],
            fwd_send,
            fwd_recv,
            (2 * c + 1 - p, local),
        )
    wait(hbuf, hid_recv)
    wait(gbuf.at[span((1 - p) * half, half)], fwd_recv)

    chunk = min(128, rows)
    many = rows // chunk
    group = chunk // piece

    def turn(r):
        return (c // group + r) % many

    def grad_chunk(r):
        at = turn(r)
        acc = lax.dot_general(
            hbuf[:, lanes(at * chunk, chunk)],
            gbuf[...],
            (((0,), (0,)), ((), ())),
            preferred_element_type=jnp.float32,
        )
        for b in range(2):
            for j in range(group):
                part_of = acc[j * piece : (j + 1) * piece, b * cols : (b + 1) * cols]
                top = jnp.max(jnp.abs(part_of), axis=0, keepdims=True)
                top = functools.reduce(
                    jnp.maximum, [top[:, k : k + 128] for k in range(0, cols, 128)]
                )
                step = jnp.maximum(top, 1e-30) * (1.0 / 32767.0)
                inverse = 1.0 / step
                coded = jnp.round(part_of * jnp.tile(inverse, (1, cols // 128)))
                coded = jnp.clip(coded, -32767.0, 32767.0)
                slot = b * copies + at * group + j
                gsend[slot] = coded.astype(jnp.int32).astype(jnp.int16)
                qsend[slot] = step

    def grad_send(r):
        at = turn(r)

        def one(i, carry):
            there = at * group + (c + i) % group
            for flip in (1, 0):
                b = (zh + flip) % 2
                to_self = (there == c) & (flip == 0)
                slot = gsend.at[b * copies + there]
                home = grecv.at[zh * copies + c]
                scale = qsend.at[b * copies + there]
                scale_home = qrecv.at[zh * copies + c]

                @pl.when(jnp.logical_not(to_self))
                def _():
                    where = (2 * there + p, b * ring + x)
                    remote(slot, home, g_send, g_recv, where)
                    remote(scale, scale_home, q_send, q_recv, where)

                if flip == 0:

                    @pl.when(to_self)
                    def _():
                        pltpu.make_async_copy(slot, home, g_recv).start()
                        pltpu.make_async_copy(scale, scale_home, q_recv).start()

            return carry

        lax.fori_loop(0, group, one, 0)

    for r in range(many):
        grad_chunk(r)
        if r >= 1:
            grad_send(r - 1)
    remote(
        w_ref,
        wbuf.at[:, lanes(zh * cols, cols)],
        w_send,
        w_recv.at[1],
        (node, (1 - zh) * ring + x),
    )
    pltpu.make_async_copy(
        w_ref, wbuf.at[:, lanes(zh * cols, cols)], w_recv.at[0]
    ).start()
    grad_send(many - 1)

    wait(sbuf, in_recv)
    wait(grecv, g_recv)
    wait(qrecv, q_recv)

    def decoded(j):
        step = jnp.tile(qrecv[j], (1, cols // 128))
        return grecv[j].astype(jnp.int32).astype(jnp.float32) * step

    def add_halves(j, carry):
        gsum[j] = decoded(j) + decoded(copies + j)
        return carry

    lax.fori_loop(0, copies, add_halves, 0)

    def update(k):
        there = other(k)
        src = source_ref[there]
        expert = holder_ref[src]

        def add(j, total):
            return total + jnp.where(holder_ref[j] == expert, 1.0, 0.0) * gsum[j]

        total = lax.fori_loop(
            0, copies, add, jnp.zeros((piece, cols), jnp.float32), unroll=4
        )
        new = adamw_step(
            total,
            sbuf[0, src].astype(jnp.float32),
            sbuf[1, src].astype(jnp.float32),
            sbuf[2, src].astype(jnp.float32),
        )
        for a in range(3):
            sout[a, there] = new[a].astype(jnp.bfloat16)

    def send_update(k):
        there = other(k)
        for a in range(3):
            remote(
                sout.at[a, there],
                outs[a].at[span(c * piece, piece)],
                out_send,
                out_recv.at[a],
                (2 * there + p, local),
            )

    update(1)

    def update_step(k, carry):
        update(k)
        send_update(k - 1)
        return carry

    lax.fori_loop(2, copies, update_step, 0)
    update(0)
    send_update(copies - 1)

    for b in range(2):
        wait(wbuf.at[:, pl.ds(b * cols, cols)], w_recv.at[b])
    for a in range(3):
        pltpu.make_async_copy(
            sout.at[a, c], outs[a].at[span(c * piece, piece)], out_recv.at[a]
        ).start()
    block = min(256, 2 * half)

    def back_chunk(i, carry):
        here = span(i * block, block)
        part[here] = lax.dot_general(
            gbuf[here],
            wbuf[...],
            (((1,), (1,)), ((), ())),
            preferred_element_type=jnp.float32,
        )
        return carry

    lax.fori_loop(0, 2 * half // block, back_chunk, 0)
    for dx in hops:
        xx = (x + dx) % ring
        for q in range(2):
            remote(
                part.at[span((q * ring + xx) * tok, tok)],
                precv.at[dx - 1, q],
                p_send,
                p_recv,
                (node, zh * ring + xx),
            )
    wait(precv, p_recv)

    def summed(q):
        total = part[span((q * ring + x) * tok, tok)]
        for dx in hops:
            total = total + precv[dx - 1, q]
        return total.astype(jnp.bfloat16)

    back[...] = summed(1 - p)
    own = summed(p)
    hb_ref[:, lanes(p * rows, rows)] = jnp.where(alive, own, jnp.zeros_like(own))
    remote(back, brecv, b_send, b_recv, (2 * c + 1 - p, local))
    wait(brecv, b_recv)
    rest = brecv[...]
    hb_ref[:, lanes((1 - p) * rows, rows)] = jnp.where(alive, rest, jnp.zeros_like(rest))

    for a in range(3):
        wait(outs[a], out_recv.at[a])
    wait(gbuf.at[span(0, (ring - 1) * tok)], og_send)
    wait(hbuf.at[span(0, (2 * ring - 1) * tok)], hid_send)
    wait(gbuf.at[span(0, half)], fwd_send)
    wait(sbuf.at[:, pl.ds(0, copies - 1)], in_send)
    wait(wbuf.at[:, pl.ds(0, cols)], w_send)
    wait(gsend.at[pl.ds(0, 2 * copies - 1)], g_send)
    wait(qsend.at[pl.ds(0, 2 * copies - 1)], q_send)
    wait(sout.at[:, pl.ds(0, copies - 1)], out_send)
    wait(precv, p_send)
    wait(brecv, b_send)


def shards(hidden_acts, out_grad, weight, first, second, holder, source, live):
    copies = lax.axis_size("node") // 2
    ring = lax.axis_size("local") // 2
    tok, hid = hidden_acts.shape
    rows, cols = weight.shape
    piece = rows // copies
    half = ring * tok
    smem = pl.BlockSpec(memory_space=pltpu.SMEM)
    vmem = pl.BlockSpec(memory_space=pltpu.VMEM)
    far = pl.BlockSpec(memory_space=pl.ANY)
    dma = pltpu.SemaphoreType.DMA
    bf16, f32 = jnp.bfloat16, jnp.float32
    state = jax.ShapeDtypeStruct((rows, cols), bf16)
    return pl.pallas_call(
        functools.partial(step_kernel, copies, ring),
        out_shape=(state, state, state, jax.ShapeDtypeStruct((tok, hid), bf16)),
        in_specs=[smem, smem, smem, vmem, far, far, far, far],
        out_specs=(far, far, far, vmem),
        scratch_shapes=[
            pltpu.VMEM((tok, hid), bf16),
            pltpu.VMEM((2 * half, rows), bf16),
            pltpu.VMEM((2 * half, 2 * cols), bf16),
            pltpu.VMEM((3, copies, piece, cols), bf16),
            pltpu.VMEM((rows, 2 * cols), bf16),
            pltpu.VMEM((2 * copies, piece, cols), jnp.int16),
            pltpu.VMEM((2 * copies, piece, cols), jnp.int16),
            pltpu.VMEM((2 * copies, 1, 128), f32),
            pltpu.VMEM((2 * copies, 1, 128), f32),
            pltpu.VMEM((copies, piece, cols), f32),
            pltpu.VMEM((3, copies, piece, cols), bf16),
            pltpu.VMEM((2 * half, rows), f32),
            pltpu.VMEM((ring - 1, 2, tok, rows), f32),
            pltpu.VMEM((tok, rows), bf16),
            pltpu.VMEM((tok, rows), bf16),
            dma,
            dma((ring,)),
            dma,
            dma,
            dma,
            dma,
            dma,
            dma,
            dma,
            dma((2,)),
            dma,
            dma,
            dma,
            dma,
            dma,
            dma,
            dma,
            dma,
            dma,
            dma((3,)),
        ],
        compiler_params=pltpu.CompilerParams(
            collective_id=0, has_side_effects=True, vmem_limit_bytes=63_000_000
        ),
    )(live, holder, source, hidden_acts, out_grad, weight, first, second)


def solution(mesh):
    token, split = P(("node", "local"), None), P("node", "local")
    return jax.shard_map(
        shards,
        mesh=mesh,
        in_specs=(token, token, split, split, split, P(), P(), split),
        out_specs=(split, split, split, token),
        check_vma=False,
    )
```

```python
import functools

import jax
import jax.numpy as jnp
from jax import lax
from jax.experimental import pallas as pl
from jax.experimental.pallas import tpu as pltpu
from jax.sharding import PartitionSpec as P

ROW_BLOCK = 32
MESH = pl.DeviceIdType.MESH

beta_one = 0.9
beta_two = 0.95
learn_rate = 0.002
decay_rate = 0.1
adam_eps = 1e-08
step_count = 10.0


def adamw_step(gradient, weight, first, second):
    first_new = beta_one * first + (1.0 - beta_one) * gradient
    second_new = beta_two * second + (1.0 - beta_two) * gradient * gradient
    update = (
        first_new
        / (1.0 - beta_one**step_count)
        / (jnp.sqrt(second_new / (1.0 - beta_two**step_count)) + adam_eps)
    )
    weight_new = weight - learn_rate * (update + decay_rate * weight)
    return weight_new, first_new, second_new


def step_kernel(
    copies,
    ring,
    live_ref,
    holder_ref,
    source_ref,
    hid_ref,
    og_ref,
    w_ref,
    m1_ref,
    m2_ref,
    out_ref,
    hb_ref,
    hid_m,
    stage,
    hbuf,
    gbuf,
    sbuf,
    wbuf,
    gsend,
    grecv,
    qsend,
    qrecv,
    gsum,
    sout,
    part,
    precv,
    back,
    brecv,
    og_send,
    og_recv,
    hid_send,
    hid_recv,
    fwd_send,
    fwd_recv,
    stage_sem,
    in_send,
    in_recv,
    w_send,
    w_recv,
    g_send,
    g_recv,
    q_send,
    q_recv,
    p_send,
    p_recv,
    b_send,
    b_recv,
    out_send,
    out_recv,
):
    tok = hid_ref.shape[0]
    piece, cols = w_ref.shape[1:]
    rows = copies * piece
    half = ring * tok
    node = lax.axis_index("node")
    local = lax.axis_index("local")
    c, p = node // 2, node % 2
    zh, x = local // ring, local % ring

    def remote(src, dst, send, recv, where):
        pltpu.make_async_remote_copy(
            src_ref=src,
            dst_ref=dst,
            send_sem=send,
            recv_sem=recv,
            device_id=where,
            device_id_type=MESH,
        ).start()

    def wait(ref, sem):
        pltpu.make_async_copy(ref, ref, sem).wait()

    def lanes(start, size):
        return pl.ds(pl.multiple_of(start, 128), size)

    def span(start, size):
        return pl.ds(pl.multiple_of(start, 16), size)

    def other(k):
        return (c + 13 * k) % copies

    def greet(where):
        pl.semaphore_signal(barrier, inc=1, device_id=where, device_id_type=MESH)

    hops = [dx for pair in zip(range(1, ring), range(ring - 1, 0, -1)) for dx in pair]
    hops = list(dict.fromkeys(hops))
    states = (w_ref, m1_ref, m2_ref)
    mine = span((p * ring + x) * tok, tok)

    barrier = pltpu.get_barrier_semaphore()

    def greet_far(k, carry):
        greet((2 * other(k) + p, (1 - zh) * ring + x))
        return carry

    def greet_near(k, carry):
        greet((2 * other(k) + p, local))
        return carry

    lax.fori_loop(0, copies, greet_far, 0)
    lax.fori_loop(1, copies, greet_near, 0)
    for dx in hops:
        for q in range(2):
            greet((2 * c + q, zh * ring + (x + dx) % ring))
    greet((2 * c + 1 - p, local))

    live = live_ref[0, 0] * ROW_BLOCK
    alive = lax.broadcasted_iota(jnp.int32, (tok, 1), 0) < live
    hid_m[...] = jnp.where(alive, hid_ref[...], jnp.zeros_like(hid_ref))
    for b in range(2):
        pltpu.make_async_copy(
            og_ref.at[:, lanes((b * ring + x) * cols, cols)],
            gbuf.at[mine, pl.ds(b * cols, cols)],
            og_recv.at[0],
        ).start()
    for a in range(3):
        pltpu.make_async_copy(states[a], stage.at[:, a], stage_sem.at[a]).start()
    pltpu.make_async_copy(
        w_ref, wbuf.at[:, :, lanes(zh * cols, cols)], w_recv.at[0]
    ).start()
    for a in range(3):
        wait(stage.at[:, a], stage_sem.at[a])
    pltpu.make_async_copy(stage.at[c], sbuf.at[c], in_recv).start()
    pl.semaphore_wait(barrier, 2 * copies + 2 * (ring - 1))

    for dx in hops:
        there = zh * ring + (x + dx) % ring
        for b in range(2):
            remote(
                og_ref.at[:, lanes((b * ring + (x + dx) % ring) * cols, cols)],
                gbuf.at[mine, pl.ds(b * cols, cols)],
                og_send,
                og_recv.at[dx],
                (node, there),
            )
        for q in range(2):
            remote(
                hid_m.at[:, pl.ds(q * rows, rows)],
                hbuf.at[mine],
                hid_send,
                hid_recv,
                (2 * c + q, there),
            )
    remote(
        hid_m.at[:, lanes((1 - p) * rows, rows)],
        hbuf.at[mine],
        hid_send,
        hid_recv,
        (2 * c + 1 - p, local),
    )
    pltpu.make_async_copy(
        hid_m.at[:, lanes(p * rows, rows)], hbuf.at[mine], hid_recv
    ).start()

    share = copies // 4
    for k in range(4):
        some = pl.ds(k * share, share)
        remote(
            stage.at[some, 0],
            wbuf.at[some, :, lanes(zh * cols, cols)],
            w_send,
            w_recv.at[1],
            (node, (1 - zh) * ring + x),
        )

    def send_states(k, carry):
        there = other(k)
        remote(stage.at[there], sbuf.at[c], in_send, in_recv, (2 * there + p, local))
        return carry

    lax.fori_loop(1, copies, send_states, 0)

    for dx in [0] + hops:
        theirs = span((p * ring + (x + ring - dx) % ring) * tok, tok)
        wait(gbuf.at[theirs], og_recv.at[dx])
        remote(
            gbuf.at[theirs],
            gbuf.at[theirs],
            fwd_send,
            fwd_recv,
            (2 * c + 1 - p, local),
        )
    wait(hbuf, hid_recv)
    wait(gbuf.at[span((1 - p) * half, half)], fwd_recv)

    chunk = min(128, rows)
    many = rows // chunk
    group = chunk // piece

    def turn(r):
        return (c // group + r) % many

    def grad_chunk(r):
        at = turn(r)
        acc = lax.dot_general(
            hbuf[:, lanes(at * chunk, chunk)],
            gbuf[...],
            (((0,), (0,)), ((), ())),
            preferred_element_type=jnp.float32,
        )
        for b in range(2):
            for j in range(group):
                part_of = acc[j * piece : (j + 1) * piece, b * cols : (b + 1) * cols]
                top = jnp.max(jnp.abs(part_of), axis=0, keepdims=True)
                top = functools.reduce(
                    jnp.maximum, [top[:, k : k + 128] for k in range(0, cols, 128)]
                )
                step = jnp.maximum(top, 1e-30) * (1.0 / 32767.0)
                inverse = 1.0 / step
                coded = jnp.round(part_of * jnp.tile(inverse, (1, cols // 128)))
                coded = jnp.clip(coded, -32767.0, 32767.0)
                slot = b * copies + at * group + j
                gsend[slot] = coded.astype(jnp.int32).astype(jnp.int16)
                qsend[slot] = step

    def grad_send(r):
        at = turn(r)

        def one(i, carry):
            there = at * group + (c + i) % group
            for flip in (1, 0):
                b = (zh + flip) % 2
                to_self = (there == c) & (flip == 0)
                slot = gsend.at[b * copies + there]
                home = grecv.at[zh * copies + c]
                scale = qsend.at[b * copies + there]
                scale_home = qrecv.at[zh * copies + c]

                @pl.when(jnp.logical_not(to_self))
                def _():
                    where = (2 * there + p, b * ring + x)
                    remote(slot, home, g_send, g_recv, where)
                    remote(scale, scale_home, q_send, q_recv, where)

                if flip == 0:

                    @pl.when(to_self)
                    def _():
                        pltpu.make_async_copy(slot, home, g_recv).start()
                        pltpu.make_async_copy(scale, scale_home, q_recv).start()

            return carry

        lax.fori_loop(0, group, one, 0)

    for r in range(many):
        grad_chunk(r)
        if r >= 1:
            grad_send(r - 1)
    grad_send(many - 1)

    wait(wbuf.at[:, :, pl.ds(0, cols)], w_recv.at[0])
    wait(wbuf.at[:, :, pl.ds(0, cols)], w_recv.at[1])
    block = min(256, 2 * half)

    def back_chunk(i, carry):
        here = span(i * block, block)
        part[here] = lax.dot_general(
            gbuf[here],
            wbuf[...].reshape(rows, 2 * cols),
            (((1,), (1,)), ((), ())),
            preferred_element_type=jnp.float32,
        )
        return carry

    lax.fori_loop(0, 2 * half // block, back_chunk, 0)
    for dx in hops:
        xx = (x + dx) % ring
        for q in range(2):
            remote(
                part.at[span((q * ring + xx) * tok, tok)],
                precv.at[dx - 1, q],
                p_send,
                p_recv,
                (node, zh * ring + xx),
            )

    wait(sbuf, in_recv)
    wait(grecv, g_recv)
    wait(qrecv, q_recv)

    def decoded(j):
        step = jnp.tile(qrecv[j], (1, cols // 128))
        return grecv[j].astype(jnp.int32).astype(jnp.float32) * step

    def add_halves(j, carry):
        gsum[j] = decoded(j) + decoded(copies + j)
        return carry

    lax.fori_loop(0, copies, add_halves, 0)

    def update(k):
        there = other(k)
        src = source_ref[there]
        expert = holder_ref[src]

        def add(j, total):
            return total + jnp.where(holder_ref[j] == expert, 1.0, 0.0) * gsum[j]

        total = lax.fori_loop(
            0, copies, add, jnp.zeros((piece, cols), jnp.float32), unroll=4
        )
        new = adamw_step(
            total,
            sbuf[src, 0].astype(jnp.float32),
            sbuf[src, 1].astype(jnp.float32),
            sbuf[src, 2].astype(jnp.float32),
        )
        for a in range(3):
            sout[there, a] = new[a].astype(jnp.bfloat16)

    def send_update(k):
        there = other(k)
        remote(sout.at[there], out_ref.at[c], out_send, out_recv, (2 * there + p, local))

    update(1)

    def update_step(k, carry):
        update(k)
        send_update(k - 1)
        return carry

    lax.fori_loop(2, copies, update_step, 0)
    update(0)
    send_update(copies - 1)

    pltpu.make_async_copy(sout.at[c], out_ref.at[c], out_recv).start()

    wait(precv, p_recv)

    def summed(q):
        total = part[span((q * ring + x) * tok, tok)]
        for dx in hops:
            total = total + precv[dx - 1, q]
        return total.astype(jnp.bfloat16)

    back[...] = summed(1 - p)
    own = summed(p)
    hb_ref[:, lanes(p * rows, rows)] = jnp.where(alive, own, jnp.zeros_like(own))
    remote(back, brecv, b_send, b_recv, (2 * c + 1 - p, local))
    wait(brecv, b_recv)
    rest = brecv[...]
    hb_ref[:, lanes((1 - p) * rows, rows)] = jnp.where(alive, rest, jnp.zeros_like(rest))

    wait(out_ref, out_recv)
    wait(gbuf.at[span(0, (ring - 1) * tok)], og_send)
    wait(hbuf.at[span(0, (2 * ring - 1) * tok)], hid_send)
    wait(gbuf.at[span(0, half)], fwd_send)
    wait(sbuf.at[pl.ds(0, copies - 1)], in_send)
    wait(wbuf.at[:, :, pl.ds(0, cols)], w_send)
    wait(gsend.at[pl.ds(0, 2 * copies - 1)], g_send)
    wait(qsend.at[pl.ds(0, 2 * copies - 1)], q_send)
    wait(sout.at[pl.ds(0, copies - 1)], out_send)
    wait(precv, p_send)
    wait(brecv, b_send)


def shards(hidden_acts, out_grad, weight, first, second, holder, source, live):
    copies = lax.axis_size("node") // 2
    ring = lax.axis_size("local") // 2
    tok, hid = hidden_acts.shape
    rows, cols = weight.shape
    piece = rows // copies
    half = ring * tok
    smem = pl.BlockSpec(memory_space=pltpu.SMEM)
    vmem = pl.BlockSpec(memory_space=pltpu.VMEM)
    far = pl.BlockSpec(memory_space=pl.ANY)
    dma = pltpu.SemaphoreType.DMA
    bf16, f32 = jnp.bfloat16, jnp.float32
    blocks = (copies, piece, cols)
    state, back = pl.pallas_call(
        functools.partial(step_kernel, copies, ring),
        out_shape=(
            jax.ShapeDtypeStruct((copies, 3, piece, cols), bf16),
            jax.ShapeDtypeStruct((tok, hid), bf16),
        ),
        in_specs=[smem, smem, smem, vmem, far, far, far, far],
        out_specs=(far, vmem),
        scratch_shapes=[
            pltpu.VMEM((tok, hid), bf16),
            pltpu.VMEM((copies, 3, piece, cols), bf16),
            pltpu.VMEM((2 * half, rows), bf16),
            pltpu.VMEM((2 * half, 2 * cols), bf16),
            pltpu.VMEM((copies, 3, piece, cols), bf16),
            pltpu.VMEM((copies, piece, 2 * cols), bf16),
            pltpu.VMEM((2 * copies, piece, cols), jnp.int16),
            pltpu.VMEM((2 * copies, piece, cols), jnp.int16),
            pltpu.VMEM((2 * copies, 1, 128), f32),
            pltpu.VMEM((2 * copies, 1, 128), f32),
            pltpu.VMEM((copies, piece, cols), f32),
            pltpu.VMEM((copies, 3, piece, cols), bf16),
            pltpu.VMEM((2 * half, rows), f32),
            pltpu.VMEM((ring - 1, 2, tok, rows), f32),
            pltpu.VMEM((tok, rows), bf16),
            pltpu.VMEM((tok, rows), bf16),
            dma,
            dma((ring,)),
            dma,
            dma,
            dma,
            dma,
            dma((3,)),
            dma,
            dma,
            dma,
            dma((2,)),
            dma,
            dma,
            dma,
            dma,
            dma,
            dma,
            dma,
            dma,
            dma,
            dma,
        ],
        compiler_params=pltpu.CompilerParams(
            collective_id=0, has_side_effects=True, vmem_limit_bytes=63_000_000
        ),
    )(
        live,
        holder,
        source,
        hidden_acts,
        out_grad,
        weight.reshape(blocks),
        first.reshape(blocks),
        second.reshape(blocks),
    )
    weight_new, first_new, second_new = (
        state[:, a].reshape(rows, cols) for a in range(3)
    )
    return weight_new, first_new, second_new, back


def solution(mesh):
    token, split = P(("node", "local"), None), P("node", "local")
    return jax.shard_map(
        shards,
        mesh=mesh,
        in_specs=(token, token, split, split, split, P(), P(), split),
        out_specs=(split, split, split, token),
        check_vma=False,
    )
```

```python
import functools

import jax
import jax.numpy as jnp
from jax import lax
from jax.experimental import pallas as pl
from jax.experimental.pallas import tpu as pltpu
from jax.sharding import PartitionSpec as P

ROW_BLOCK = 32
PARTS = 4
MESH = pl.DeviceIdType.MESH

beta_one = 0.9
beta_two = 0.95
learn_rate = 0.002
decay_rate = 0.1
adam_eps = 1e-08
step_count = 10.0


def adamw_step(gradient, weight, first, second):
    first_new = beta_one * first + (1.0 - beta_one) * gradient
    second_new = beta_two * second + (1.0 - beta_two) * gradient * gradient
    update = (
        first_new
        / (1.0 - beta_one**step_count)
        / (jnp.sqrt(second_new / (1.0 - beta_two**step_count)) + adam_eps)
    )
    weight_new = weight - learn_rate * (update + decay_rate * weight)
    return weight_new, first_new, second_new


def step_kernel(
    copies,
    ring,
    live_ref,
    holder_ref,
    source_ref,
    hid_ref,
    og_ref,
    w_ref,
    m1_ref,
    m2_ref,
    out_ref,
    hb_ref,
    hid_m,
    stage,
    hbuf,
    gbuf,
    sbuf,
    wbuf,
    gsend,
    grecv,
    qsend,
    qrecv,
    gsum,
    sout,
    part,
    precv,
    back,
    brecv,
    og_send,
    og_recv,
    hid_send,
    hid_recv,
    fwd_send,
    fwd_recv,
    stage_sem,
    in_send,
    in_recv,
    w_send,
    w_recv,
    g_send,
    g_recv,
    q_send,
    q_recv,
    p_send,
    p_recv,
    b_send,
    b_recv,
    out_send,
    out_recv,
):
    tok = hid_ref.shape[0]
    piece, cols = w_ref.shape[1:]
    rows = copies * piece
    half = ring * tok
    wide = cols // 2
    node = lax.axis_index("node")
    local = lax.axis_index("local")
    c, p = node // 2, node % 2
    zh, x = local // ring, local % ring

    def remote(src, dst, send, recv, where):
        pltpu.make_async_remote_copy(
            src_ref=src,
            dst_ref=dst,
            send_sem=send,
            recv_sem=recv,
            device_id=where,
            device_id_type=MESH,
        ).start()

    def wait(ref, sem):
        pltpu.make_async_copy(ref, ref, sem).wait()

    def lanes(start, size):
        return pl.ds(pl.multiple_of(start, 128), size)

    def span(start, size):
        return pl.ds(pl.multiple_of(start, 16), size)

    def other(k):
        return (c + 13 * k) % copies

    def greet(where):
        pl.semaphore_signal(barrier, inc=1, device_id=where, device_id_type=MESH)

    hops = [dx for pair in zip(range(1, ring), range(ring - 1, 0, -1)) for dx in pair]
    hops = list(dict.fromkeys(hops))
    states = (w_ref, m1_ref, m2_ref)
    mine = span((p * ring + x) * tok, tok)

    barrier = pltpu.get_barrier_semaphore()

    def greet_far(k, carry):
        greet((2 * other(k) + p, (1 - zh) * ring + x))
        return carry

    def greet_near(k, carry):
        greet((2 * other(k) + p, local))
        return carry

    lax.fori_loop(0, copies, greet_far, 0)
    lax.fori_loop(1, copies, greet_near, 0)
    for dx in hops:
        for q in range(2):
            greet((2 * c + q, zh * ring + (x + dx) % ring))
    greet((2 * c + 1 - p, local))

    live = live_ref[0, 0] * ROW_BLOCK
    alive = lax.broadcasted_iota(jnp.int32, (tok, 1), 0) < live
    hid_m[...] = jnp.where(alive, hid_ref[...], jnp.zeros_like(hid_ref))
    for b in range(2):
        pltpu.make_async_copy(
            og_ref.at[:, lanes((b * ring + x) * cols, cols)],
            gbuf.at[mine, pl.ds(b * cols, cols)],
            og_recv.at[0],
        ).start()
    for a in range(3):
        pltpu.make_async_copy(states[a], stage.at[:, a], stage_sem.at[a]).start()
    pltpu.make_async_copy(
        w_ref, wbuf.at[:, :, lanes(zh * cols, cols)], w_recv.at[0]
    ).start()
    for a in range(3):
        wait(stage.at[:, a], stage_sem.at[a])
    pltpu.make_async_copy(stage.at[c], sbuf.at[c], in_recv).start()
    pl.semaphore_wait(barrier, 2 * copies + 2 * (ring - 1))

    for dx in hops:
        there = zh * ring + (x + dx) % ring
        for b in range(2):
            remote(
                og_ref.at[:, lanes((b * ring + (x + dx) % ring) * cols, cols)],
                gbuf.at[mine, pl.ds(b * cols, cols)],
                og_send,
                og_recv.at[dx],
                (node, there),
            )
        for q in range(2):
            remote(
                hid_m.at[:, pl.ds(q * rows, rows)],
                hbuf.at[mine],
                hid_send,
                hid_recv,
                (2 * c + q, there),
            )
    remote(
        hid_m.at[:, lanes((1 - p) * rows, rows)],
        hbuf.at[mine],
        hid_send,
        hid_recv,
        (2 * c + 1 - p, local),
    )
    pltpu.make_async_copy(
        hid_m.at[:, lanes(p * rows, rows)], hbuf.at[mine], hid_recv
    ).start()

    share = copies // 4
    for k in range(4):
        some = pl.ds(k * share, share)
        remote(
            stage.at[some, 0],
            wbuf.at[some, :, lanes(zh * cols, cols)],
            w_send,
            w_recv.at[1],
            (node, (1 - zh) * ring + x),
        )

    def send_states(k, carry):
        there = other(k)
        remote(stage.at[there], sbuf.at[c], in_send, in_recv, (2 * there + p, local))
        return carry

    lax.fori_loop(1, copies, send_states, 0)

    for dx in [0] + hops:
        theirs = span((p * ring + (x + ring - dx) % ring) * tok, tok)
        wait(gbuf.at[theirs], og_recv.at[dx])
        remote(
            gbuf.at[theirs],
            gbuf.at[theirs],
            fwd_send,
            fwd_recv,
            (2 * c + 1 - p, local),
        )
    wait(hbuf, hid_recv)
    wait(gbuf.at[span((1 - p) * half, half)], fwd_recv)

    chunk = min(128, rows)
    many = rows // chunk
    group = chunk // piece

    def turn(r):
        return (c // group + r) % many

    def grad_chunk(r):
        at = turn(r)
        acc = lax.dot_general(
            hbuf[:, lanes(at * chunk, chunk)],
            gbuf[...],
            (((0,), (0,)), ((), ())),
            preferred_element_type=jnp.float32,
        )
        for b in range(2):
            for j in range(group):
                part_of = acc[j * piece : (j + 1) * piece, b * cols : (b + 1) * cols]
                top = jnp.max(jnp.abs(part_of), axis=0, keepdims=True)
                top = functools.reduce(
                    jnp.maximum, [top[:, k : k + 128] for k in range(0, cols, 128)]
                )
                step = jnp.maximum(top, 1e-30) * (1.0 / 32767.0)
                inverse = 1.0 / step
                coded = jnp.round(part_of * jnp.tile(inverse, (1, cols // 128)))
                coded = jnp.clip(coded, -32767.0, 32767.0)
                slot = b * copies + at * group + j
                coded = coded.astype(jnp.int32).astype(jnp.int16)
                for h in range(2):
                    gsend[slot, h] = coded[:, h * wide : (h + 1) * wide]
                qsend[slot] = step

    def grad_send(r, h):
        at = turn(r)

        def one(i, carry):
            there = at * group + (c + i) % group
            for flip in (1, 0):
                b = (zh + flip) % 2
                to_self = (there == c) & (flip == 0)
                slot = gsend.at[b * copies + there, h]
                home = grecv.at[zh * copies + c, h]
                scale = qsend.at[b * copies + there]
                scale_home = qrecv.at[zh * copies + c]

                @pl.when(jnp.logical_not(to_self))
                def _():
                    where = (2 * there + p, b * ring + x)
                    remote(slot, home, g_send, g_recv.at[h], where)
                    if h == 0:
                        remote(scale, scale_home, q_send, q_recv, where)

                if flip == 0:

                    @pl.when(to_self)
                    def _():
                        pltpu.make_async_copy(slot, home, g_recv.at[h]).start()
                        if h == 0:
                            pltpu.make_async_copy(scale, scale_home, q_recv).start()

            return carry

        lax.fori_loop(0, group, one, 0)

    for r in range(many):
        grad_chunk(r)
    for h in range(2):
        for r in range(many):
            grad_send(r, h)

    wait(wbuf.at[:, :, pl.ds(0, cols)], w_recv.at[0])
    wait(wbuf.at[:, :, pl.ds(0, cols)], w_recv.at[1])
    block = min(256, 2 * half)

    def back_chunk(i, carry):
        here = span(i * block, block)
        part[here] = lax.dot_general(
            gbuf[here],
            wbuf[...].reshape(rows, 2 * cols),
            (((1,), (1,)), ((), ())),
            preferred_element_type=jnp.float32,
        )
        return carry

    lax.fori_loop(0, 2 * half // block, back_chunk, 0)
    for dx in hops:
        xx = (x + dx) % ring
        for q in range(2):
            remote(
                part.at[span((q * ring + xx) * tok, tok)],
                precv.at[dx - 1, q],
                p_send,
                p_recv,
                (node, zh * ring + xx),
            )

    wait(sbuf, in_recv)
    wait(qrecv, q_recv)

    def update_half(h):
        part_cols = pl.ds(h * wide, wide)
        wait(grecv.at[:, h], g_recv.at[h])

        def decoded(j):
            step = jnp.tile(qrecv[j], (1, wide // 128))
            return grecv[j, h].astype(jnp.int32).astype(jnp.float32) * step

        def add_halves(j, carry):
            gsum[j] = decoded(j) + decoded(copies + j)
            return carry

        lax.fori_loop(0, copies, add_halves, 0)

        def update(k):
            there = other(k)
            src = source_ref[there]
            expert = holder_ref[src]

            def add(j, total):
                return total + jnp.where(holder_ref[j] == expert, 1.0, 0.0) * gsum[j]

            total = lax.fori_loop(
                0, copies, add, jnp.zeros((piece, wide), jnp.float32), unroll=8
            )
            new = adamw_step(
                total,
                sbuf[src, 0, :, part_cols].astype(jnp.float32),
                sbuf[src, 1, :, part_cols].astype(jnp.float32),
                sbuf[src, 2, :, part_cols].astype(jnp.float32),
            )
            for a in range(3):
                sout[there, a, :, part_cols] = new[a].astype(jnp.bfloat16)

        def send_update(k):
            there = other(k)
            remote(
                sout.at[there, :, :, part_cols],
                out_ref.at[c, :, :, part_cols],
                out_send,
                out_recv,
                (2 * there + p, local),
            )

        update(1)

        def update_step(k, carry):
            update(k)
            send_update(k - 1)
            return carry

        lax.fori_loop(2, copies, update_step, 0)
        update(0)
        send_update(copies - 1)

    update_half(0)
    update_half(1)

    pltpu.make_async_copy(sout.at[c], out_ref.at[c], out_recv).start()

    wait(precv, p_recv)

    def summed(q):
        total = part[span((q * ring + x) * tok, tok)]
        for dx in hops:
            total = total + precv[dx - 1, q]
        return total.astype(jnp.bfloat16)

    back[...] = summed(1 - p)
    own = summed(p)
    hb_ref[:, lanes(p * rows, rows)] = jnp.where(alive, own, jnp.zeros_like(own))
    remote(back, brecv, b_send, b_recv, (2 * c + 1 - p, local))
    wait(brecv, b_recv)
    rest = brecv[...]
    hb_ref[:, lanes((1 - p) * rows, rows)] = jnp.where(alive, rest, jnp.zeros_like(rest))

    wait(out_ref, out_recv)
    wait(gbuf.at[span(0, (ring - 1) * tok)], og_send)
    wait(hbuf.at[span(0, (2 * ring - 1) * tok)], hid_send)
    wait(gbuf.at[span(0, half)], fwd_send)
    wait(sbuf.at[pl.ds(0, copies - 1)], in_send)
    wait(wbuf.at[:, :, pl.ds(0, cols)], w_send)
    wait(gsend.at[pl.ds(0, 2 * copies - 1)], g_send)
    wait(qsend.at[pl.ds(0, 2 * copies - 1)], q_send)
    wait(sout.at[pl.ds(0, copies - 1)], out_send)
    wait(precv, p_send)
    wait(brecv, b_send)


def place_kernel(
    state_ref, back_ref, w_ref, m1_ref, m2_ref, hb_ref, held, held_back, came, went
):
    jobs = []
    for k in range(PARTS):
        for a, ref in enumerate((w_ref, m1_ref, m2_ref)):
            size = ref.shape[0] // PARTS
            some = pl.ds(k * size, size)
            jobs.append((state_ref.at[some, a], held.at[a, some], ref.at[some], a, k))
        size = hb_ref.shape[0] // PARTS
        some = pl.ds(k * size, size)
        jobs.append((back_ref.at[some], held_back.at[some], hb_ref.at[some], 3, k))
    first = [pltpu.make_async_copy(src, mid, came.at[a, k]) for src, mid, _, a, k in jobs]
    last = [pltpu.make_async_copy(mid, dst, went.at[a, k]) for _, mid, dst, a, k in jobs]
    for copy in first:
        copy.start()
    for copy, onward in zip(first, last):
        copy.wait()
        onward.start()
    for copy in last:
        copy.wait()


def shards(hidden_acts, out_grad, weight, first, second, holder, source, live):
    copies = lax.axis_size("node") // 2
    ring = lax.axis_size("local") // 2
    tok, hid = hidden_acts.shape
    rows, cols = weight.shape
    piece = rows // copies
    half = ring * tok
    smem = pl.BlockSpec(memory_space=pltpu.SMEM)
    vmem = pl.BlockSpec(memory_space=pltpu.VMEM)
    far = pl.BlockSpec(memory_space=pl.ANY)
    dma = pltpu.SemaphoreType.DMA
    bf16, f32 = jnp.bfloat16, jnp.float32
    blocks = (copies, piece, cols)
    state, back = pl.pallas_call(
        functools.partial(step_kernel, copies, ring),
        out_shape=(
            jax.ShapeDtypeStruct((copies, 3, piece, cols), bf16),
            jax.ShapeDtypeStruct((tok, hid), bf16),
        ),
        in_specs=[smem, smem, smem, vmem, far, far, far, far],
        out_specs=(far, vmem),
        scratch_shapes=[
            pltpu.VMEM((tok, hid), bf16),
            pltpu.VMEM((copies, 3, piece, cols), bf16),
            pltpu.VMEM((2 * half, rows), bf16),
            pltpu.VMEM((2 * half, 2 * cols), bf16),
            pltpu.VMEM((copies, 3, piece, cols), bf16),
            pltpu.VMEM((copies, piece, 2 * cols), bf16),
            pltpu.VMEM((2 * copies, 2, piece, cols // 2), jnp.int16),
            pltpu.VMEM((2 * copies, 2, piece, cols // 2), jnp.int16),
            pltpu.VMEM((2 * copies, 1, 128), f32),
            pltpu.VMEM((2 * copies, 1, 128), f32),
            pltpu.VMEM((copies, piece, cols // 2), f32),
            pltpu.VMEM((copies, 3, piece, cols), bf16),
            pltpu.VMEM((2 * half, rows), f32),
            pltpu.VMEM((ring - 1, 2, tok, rows), f32),
            pltpu.VMEM((tok, rows), bf16),
            pltpu.VMEM((tok, rows), bf16),
            dma,
            dma((ring,)),
            dma,
            dma,
            dma,
            dma,
            dma((3,)),
            dma,
            dma,
            dma,
            dma((2,)),
            dma,
            dma((2,)),
            dma,
            dma,
            dma,
            dma,
            dma,
            dma,
            dma,
            dma,
        ],
        compiler_params=pltpu.CompilerParams(
            collective_id=0, has_side_effects=True, vmem_limit_bytes=63_000_000
        ),
    )(
        live,
        holder,
        source,
        hidden_acts,
        out_grad,
        weight.reshape(blocks),
        first.reshape(blocks),
        second.reshape(blocks),
    )
    block = jax.ShapeDtypeStruct(blocks, bf16)
    weight_new, first_new, second_new, hidden_back = pl.pallas_call(
        place_kernel,
        out_shape=(block, block, block, jax.ShapeDtypeStruct((tok, hid), bf16)),
        in_specs=[far, far],
        out_specs=(far, far, far, far),
        scratch_shapes=[
            pltpu.VMEM((3, copies, piece, cols), bf16),
            pltpu.VMEM((tok, hid), bf16),
            dma((4, PARTS)),
            dma((4, PARTS)),
        ],
    )(state, back)
    return (
        weight_new.reshape(rows, cols),
        first_new.reshape(rows, cols),
        second_new.reshape(rows, cols),
        hidden_back,
    )


def solution(mesh):
    token, split = P(("node", "local"), None), P("node", "local")
    return jax.shard_map(
        shards,
        mesh=mesh,
        in_specs=(token, token, split, split, split, P(), P(), split),
        out_specs=(split, split, split, token),
        check_vma=False,
    )
```

```python
import functools

import jax
import jax.numpy as jnp
from jax import lax
from jax.experimental import pallas as pl
from jax.experimental.pallas import tpu as pltpu
from jax.sharding import PartitionSpec as P

ROW_BLOCK = 32
PARTS = 4
MESH = pl.DeviceIdType.MESH

beta_one = 0.9
beta_two = 0.95
learn_rate = 0.002
decay_rate = 0.1
adam_eps = 1e-08
step_count = 10.0


def adamw_step(gradient, weight, first, second):
    first_new = beta_one * first + (1.0 - beta_one) * gradient
    second_new = beta_two * second + (1.0 - beta_two) * gradient * gradient
    update = (
        first_new
        / (1.0 - beta_one**step_count)
        / (jnp.sqrt(second_new / (1.0 - beta_two**step_count)) + adam_eps)
    )
    weight_new = weight - learn_rate * (update + decay_rate * weight)
    return weight_new, first_new, second_new


def step_kernel(
    copies,
    ring,
    live_ref,
    holder_ref,
    source_ref,
    hid_ref,
    og_ref,
    w_ref,
    m1_ref,
    m2_ref,
    out_ref,
    hb_ref,
    hid_m,
    stage,
    hbuf,
    gbuf,
    sbuf,
    wbuf,
    gsend,
    grecv,
    qsend,
    qrecv,
    gsum,
    sout,
    part,
    precv,
    back,
    brecv,
    og_send,
    og_recv,
    hid_send,
    hid_recv,
    fwd_send,
    fwd_recv,
    stage_sem,
    in_send,
    in_recv,
    w_send,
    w_recv,
    g_send,
    g_recv,
    q_send,
    q_recv,
    p_send,
    p_recv,
    b_send,
    b_recv,
    out_send,
    out_recv,
):
    tok = hid_ref.shape[0]
    piece, cols = w_ref.shape[1:]
    rows = copies * piece
    half = ring * tok
    wide = cols // 2
    node = lax.axis_index("node")
    local = lax.axis_index("local")
    c, p = node // 2, node % 2
    zh, x = local // ring, local % ring

    def remote(src, dst, send, recv, where):
        pltpu.make_async_remote_copy(
            src_ref=src,
            dst_ref=dst,
            send_sem=send,
            recv_sem=recv,
            device_id=where,
            device_id_type=MESH,
        ).start()

    def wait(ref, sem):
        pltpu.make_async_copy(ref, ref, sem).wait()

    def lanes(start, size):
        return pl.ds(pl.multiple_of(start, 128), size)

    def span(start, size):
        return pl.ds(pl.multiple_of(start, 16), size)

    def other(k):
        return (c + 13 * k) % copies

    def greet(where):
        pl.semaphore_signal(barrier, inc=1, device_id=where, device_id_type=MESH)

    hops = [dx for pair in zip(range(1, ring), range(ring - 1, 0, -1)) for dx in pair]
    hops = list(dict.fromkeys(hops))
    states = (w_ref, m1_ref, m2_ref)
    mine = span((p * ring + x) * tok, tok)

    barrier = pltpu.get_barrier_semaphore()

    def greet_far(k, carry):
        greet((2 * other(k) + p, (1 - zh) * ring + x))
        return carry

    def greet_near(k, carry):
        greet((2 * other(k) + p, local))
        return carry

    lax.fori_loop(0, copies, greet_far, 0, unroll=8)
    lax.fori_loop(1, copies, greet_near, 0, unroll=True)
    for dx in hops:
        for q in range(2):
            greet((2 * c + q, zh * ring + (x + dx) % ring))
    greet((2 * c + 1 - p, local))

    live = live_ref[0, 0] * ROW_BLOCK
    alive = lax.broadcasted_iota(jnp.int32, (tok, 1), 0) < live
    hid_m[...] = jnp.where(alive, hid_ref[...], jnp.zeros_like(hid_ref))
    for b in range(2):
        pltpu.make_async_copy(
            og_ref.at[:, lanes((b * ring + x) * cols, cols)],
            gbuf.at[mine, pl.ds(b * cols, cols)],
            og_recv.at[0],
        ).start()
    for a in range(3):
        pltpu.make_async_copy(states[a], stage.at[:, a], stage_sem.at[a]).start()
    pltpu.make_async_copy(
        w_ref, wbuf.at[:, :, lanes(zh * cols, cols)], w_recv.at[0]
    ).start()
    for a in range(3):
        wait(stage.at[:, a], stage_sem.at[a])
    pltpu.make_async_copy(stage.at[c], sbuf.at[c], in_recv).start()
    pl.semaphore_wait(barrier, 2 * copies + 2 * (ring - 1))

    for dx in hops:
        there = zh * ring + (x + dx) % ring
        for b in range(2):
            remote(
                og_ref.at[:, lanes((b * ring + (x + dx) % ring) * cols, cols)],
                gbuf.at[mine, pl.ds(b * cols, cols)],
                og_send,
                og_recv.at[dx],
                (node, there),
            )
        for q in range(2):
            remote(
                hid_m.at[:, pl.ds(q * rows, rows)],
                hbuf.at[mine],
                hid_send,
                hid_recv,
                (2 * c + q, there),
            )
    remote(
        hid_m.at[:, lanes((1 - p) * rows, rows)],
        hbuf.at[mine],
        hid_send,
        hid_recv,
        (2 * c + 1 - p, local),
    )
    pltpu.make_async_copy(
        hid_m.at[:, lanes(p * rows, rows)], hbuf.at[mine], hid_recv
    ).start()

    share = copies // 4
    for k in range(4):
        some = pl.ds(k * share, share)
        remote(
            stage.at[some, 0],
            wbuf.at[some, :, lanes(zh * cols, cols)],
            w_send,
            w_recv.at[1],
            (node, (1 - zh) * ring + x),
        )

    def send_states(k, carry):
        there = other(k)
        remote(stage.at[there], sbuf.at[c], in_send, in_recv, (2 * there + p, local))
        return carry

    lax.fori_loop(1, copies, send_states, 0)

    for dx in [0] + hops:
        theirs = span((p * ring + (x + ring - dx) % ring) * tok, tok)
        wait(gbuf.at[theirs], og_recv.at[dx])
        remote(
            gbuf.at[theirs],
            gbuf.at[theirs],
            fwd_send,
            fwd_recv,
            (2 * c + 1 - p, local),
        )
    wait(hbuf, hid_recv)
    wait(gbuf.at[span((1 - p) * half, half)], fwd_recv)

    chunk = min(128, rows)
    many = rows // chunk
    group = chunk // piece

    def turn(r):
        return (c // group + r) % many

    def grad_chunk(r):
        at = turn(r)
        acc = lax.dot_general(
            hbuf[:, lanes(at * chunk, chunk)],
            gbuf[...],
            (((0,), (0,)), ((), ())),
            preferred_element_type=jnp.float32,
        )
        for b in range(2):
            for j in range(group):
                part_of = acc[j * piece : (j + 1) * piece, b * cols : (b + 1) * cols]
                top = jnp.max(jnp.abs(part_of), axis=0, keepdims=True)
                top = functools.reduce(
                    jnp.maximum, [top[:, k : k + 128] for k in range(0, cols, 128)]
                )
                step = jnp.maximum(top, 1e-30) * (1.0 / 32767.0)
                inverse = 1.0 / step
                coded = jnp.round(part_of * jnp.tile(inverse, (1, cols // 128)))
                coded = jnp.clip(coded, -32767.0, 32767.0)
                slot = b * copies + at * group + j
                coded = coded.astype(jnp.int32).astype(jnp.int16)
                for h in range(2):
                    gsend[slot, h] = coded[:, h * wide : (h + 1) * wide]
                qsend[slot] = step

    def grad_send(h):
        def one(i, carry):
            there = other(i)
            for flip in (1, 0):
                b = (zh + flip) % 2
                to_self = (there == c) & (flip == 0)
                slot = gsend.at[b * copies + there, h]
                home = grecv.at[zh * copies + c, h]
                scale = qsend.at[b * copies + there]
                scale_home = qrecv.at[zh * copies + c]

                @pl.when(jnp.logical_not(to_self))
                def _():
                    where = (2 * there + p, b * ring + x)
                    remote(slot, home, g_send, g_recv.at[h], where)
                    if h == 0:
                        remote(scale, scale_home, q_send, q_recv, where)

                if flip == 0:

                    @pl.when(to_self)
                    def _():
                        pltpu.make_async_copy(slot, home, g_recv.at[h]).start()
                        if h == 0:
                            pltpu.make_async_copy(scale, scale_home, q_recv).start()

            return carry

        lax.fori_loop(0, copies, one, 0)

    for r in range(many):
        grad_chunk(r)
    for h in range(2):
        grad_send(h)

    wait(wbuf.at[:, :, pl.ds(0, cols)], w_recv.at[0])
    wait(wbuf.at[:, :, pl.ds(0, cols)], w_recv.at[1])
    block = min(256, 2 * half)

    def back_chunk(i, carry):
        here = span(i * block, block)
        part[here] = lax.dot_general(
            gbuf[here],
            wbuf[...].reshape(rows, 2 * cols),
            (((1,), (1,)), ((), ())),
            preferred_element_type=jnp.float32,
        )
        return carry

    lax.fori_loop(0, 2 * half // block, back_chunk, 0)
    for dx in hops:
        xx = (x + dx) % ring
        for q in range(2):
            remote(
                part.at[span((q * ring + xx) * tok, tok)],
                precv.at[dx - 1, q],
                p_send,
                p_recv,
                (node, zh * ring + xx),
            )

    wait(sbuf, in_recv)
    wait(qrecv, q_recv)

    def update_half(h):
        part_cols = pl.ds(h * wide, wide)
        wait(grecv.at[:, h], g_recv.at[h])

        def decoded(j):
            step = jnp.tile(qrecv[j], (1, wide // 128))
            return grecv[j, h].astype(jnp.int32).astype(jnp.float32) * step

        def add_halves(j, carry):
            gsum[j] = decoded(j) + decoded(copies + j)
            return carry

        lax.fori_loop(0, copies, add_halves, 0)

        def update(k):
            there = other(k)
            src = source_ref[there]
            expert = holder_ref[src]

            def add(j, total):
                return total + jnp.where(holder_ref[j] == expert, 1.0, 0.0) * gsum[j]

            total = lax.fori_loop(
                0, copies, add, jnp.zeros((piece, wide), jnp.float32), unroll=8
            )
            new = adamw_step(
                total,
                sbuf[src, 0, :, part_cols].astype(jnp.float32),
                sbuf[src, 1, :, part_cols].astype(jnp.float32),
                sbuf[src, 2, :, part_cols].astype(jnp.float32),
            )
            for a in range(3):
                sout[there, a, :, part_cols] = new[a].astype(jnp.bfloat16)

        def send_update(k):
            there = other(k)
            remote(
                sout.at[there, :, :, part_cols],
                out_ref.at[c, :, :, part_cols],
                out_send,
                out_recv,
                (2 * there + p, local),
            )

        update(1)

        def update_step(k, carry):
            update(k)
            send_update(k - 1)
            return carry

        lax.fori_loop(2, copies, update_step, 0)
        update(0)
        send_update(copies - 1)

    update_half(0)
    update_half(1)

    pltpu.make_async_copy(sout.at[c], out_ref.at[c], out_recv).start()

    wait(precv, p_recv)

    def summed(q):
        total = part[span((q * ring + x) * tok, tok)]
        for dx in hops:
            total = total + precv[dx - 1, q]
        return total.astype(jnp.bfloat16)

    back[...] = summed(1 - p)
    own = summed(p)
    hb_ref[:, lanes(p * rows, rows)] = jnp.where(alive, own, jnp.zeros_like(own))
    remote(back, brecv, b_send, b_recv, (2 * c + 1 - p, local))
    wait(brecv, b_recv)
    rest = brecv[...]
    hb_ref[:, lanes((1 - p) * rows, rows)] = jnp.where(alive, rest, jnp.zeros_like(rest))

    wait(out_ref, out_recv)
    wait(gbuf.at[span(0, (ring - 1) * tok)], og_send)
    wait(hbuf.at[span(0, (2 * ring - 1) * tok)], hid_send)
    wait(gbuf.at[span(0, half)], fwd_send)
    wait(sbuf.at[pl.ds(0, copies - 1)], in_send)
    wait(wbuf.at[:, :, pl.ds(0, cols)], w_send)
    wait(gsend.at[pl.ds(0, 2 * copies - 1)], g_send)
    wait(qsend.at[pl.ds(0, 2 * copies - 1)], q_send)
    wait(sout.at[pl.ds(0, copies - 1)], out_send)
    wait(precv, p_send)
    wait(brecv, b_send)


def place_kernel(
    state_ref, back_ref, w_ref, m1_ref, m2_ref, hb_ref, held, held_back, came, went
):
    jobs = []
    for k in range(PARTS):
        for a, ref in enumerate((w_ref, m1_ref, m2_ref)):
            size = ref.shape[0] // PARTS
            some = pl.ds(k * size, size)
            jobs.append((state_ref.at[some, a], held.at[a, some], ref.at[some], a, k))
        size = hb_ref.shape[0] // PARTS
        some = pl.ds(k * size, size)
        jobs.append((back_ref.at[some], held_back.at[some], hb_ref.at[some], 3, k))
    first = [pltpu.make_async_copy(src, mid, came.at[a, k]) for src, mid, _, a, k in jobs]
    last = [pltpu.make_async_copy(mid, dst, went.at[a, k]) for _, mid, dst, a, k in jobs]
    for copy in first:
        copy.start()
    for copy, onward in zip(first, last):
        copy.wait()
        onward.start()
    for copy in last:
        copy.wait()


def shards(hidden_acts, out_grad, weight, first, second, holder, source, live):
    copies = lax.axis_size("node") // 2
    ring = lax.axis_size("local") // 2
    tok, hid = hidden_acts.shape
    rows, cols = weight.shape
    piece = rows // copies
    half = ring * tok
    smem = pl.BlockSpec(memory_space=pltpu.SMEM)
    vmem = pl.BlockSpec(memory_space=pltpu.VMEM)
    far = pl.BlockSpec(memory_space=pl.ANY)
    dma = pltpu.SemaphoreType.DMA
    bf16, f32 = jnp.bfloat16, jnp.float32
    blocks = (copies, piece, cols)
    state, back = pl.pallas_call(
        functools.partial(step_kernel, copies, ring),
        out_shape=(
            jax.ShapeDtypeStruct((copies, 3, piece, cols), bf16),
            jax.ShapeDtypeStruct((tok, hid), bf16),
        ),
        in_specs=[smem, smem, smem, vmem, far, far, far, far],
        out_specs=(far, vmem),
        scratch_shapes=[
            pltpu.VMEM((tok, hid), bf16),
            pltpu.VMEM((copies, 3, piece, cols), bf16),
            pltpu.VMEM((2 * half, rows), bf16),
            pltpu.VMEM((2 * half, 2 * cols), bf16),
            pltpu.VMEM((copies, 3, piece, cols), bf16),
            pltpu.VMEM((copies, piece, 2 * cols), bf16),
            pltpu.VMEM((2 * copies, 2, piece, cols // 2), jnp.int16),
            pltpu.VMEM((2 * copies, 2, piece, cols // 2), jnp.int16),
            pltpu.VMEM((2 * copies, 1, 128), f32),
            pltpu.VMEM((2 * copies, 1, 128), f32),
            pltpu.VMEM((copies, piece, cols // 2), f32),
            pltpu.VMEM((copies, 3, piece, cols), bf16),
            pltpu.VMEM((2 * half, rows), f32),
            pltpu.VMEM((ring - 1, 2, tok, rows), f32),
            pltpu.VMEM((tok, rows), bf16),
            pltpu.VMEM((tok, rows), bf16),
            dma,
            dma((ring,)),
            dma,
            dma,
            dma,
            dma,
            dma((3,)),
            dma,
            dma,
            dma,
            dma((2,)),
            dma,
            dma((2,)),
            dma,
            dma,
            dma,
            dma,
            dma,
            dma,
            dma,
            dma,
        ],
        compiler_params=pltpu.CompilerParams(
            collective_id=0, has_side_effects=True, vmem_limit_bytes=63_000_000
        ),
    )(
        live,
        holder,
        source,
        hidden_acts,
        out_grad,
        weight.reshape(blocks),
        first.reshape(blocks),
        second.reshape(blocks),
    )
    block = jax.ShapeDtypeStruct(blocks, bf16)
    weight_new, first_new, second_new, hidden_back = pl.pallas_call(
        place_kernel,
        out_shape=(block, block, block, jax.ShapeDtypeStruct((tok, hid), bf16)),
        in_specs=[far, far],
        out_specs=(far, far, far, far),
        scratch_shapes=[
            pltpu.VMEM((3, copies, piece, cols), bf16),
            pltpu.VMEM((tok, hid), bf16),
            dma((4, PARTS)),
            dma((4, PARTS)),
        ],
    )(state, back)
    return (
        weight_new.reshape(rows, cols),
        first_new.reshape(rows, cols),
        second_new.reshape(rows, cols),
        hidden_back,
    )


def solution(mesh):
    token, split = P(("node", "local"), None), P("node", "local")
    return jax.shard_map(
        shards,
        mesh=mesh,
        in_specs=(token, token, split, split, split, P(), P(), split),
        out_specs=(split, split, split, token),
        check_vma=False,
    )
```
